32 devices in a mesh: tm: 8 (over y, x, core), space: 4 (over z).
Axes of the slice: x: 2, y: 2, z: 4, core: 2. Of those that a mesh axis runs over, the one named last changes fastest.
Arguments:
- frames: bfloat16 [128, 256, 768], P('tm', 'space'), may hold values from -6 to 6
- gain_time: float32 [768], replicated, may hold values from 0.25 to 1.75
- wq_time: bfloat16 [768, 768], replicated, may hold values from -6 to 6
- wkv_time: bfloat16 [768, 512], replicated, may hold values from -6 to 6
- wo_time: bfloat16 [768, 768], replicated, may hold values from -0.21875 to 0.21875
- gain_space: float32 [768], replicated, may hold values from 0.25 to 1.75
- wq_space: bfloat16 [768, 768], replicated, may hold values from -6 to 6
- wkv_space: bfloat16 [768, 512], replicated, may hold values from -6 to 6
- wo_space: bfloat16 [768, 768], replicated, may hold values from -0.21875 to 0.21875
- gain_mlp: float32 [768], replicated, may hold values from 0.25 to 1.75
- w_in: bfloat16 [768, 3072], replicated, may hold values from -0.21875 to 0.21875
- w_out: bfloat16 [3072, 768], replicated, may hold values from -0.109375 to 0.109375
Outputs:
- encoded: bfloat16 [128, 256, 768], P('tm', 'space')
The draws below stay inside these ranges and needn't reach their ends.
All inputs are finite; a program needn't handle non-finite values.
Results may differ from the reference program's by a relative error of at most 0.025.
The reference program's roundings to bfloat16 on the way count: a program that leaves them out, or rounds other values in their place, can miss the bound.
Values may be sent and summed in bfloat16 or wider, within the bound.
A program may use at most 192 MiB of HBM per device.

```python
import jax
import jax.numpy as jnp
from jax import lax

D = 768
HEADS = 12
KV_HEADS = 4
HEAD = 64
FF = 3072
WINDOW = 8
FRAMES = 128
PATCHES = 256


def projection_pair(key, label):
    base = jax.random.fold_in(key, label)
    first, second, third = jax.random.split(base, 3)
    scale = 1.0 / jnp.sqrt(jnp.float32(D))
    w_query = jax.random.normal(first, (D, HEADS * HEAD), jnp.float32) * scale
    w_keys = jax.random.normal(second, (D, KV_HEADS * HEAD), jnp.float32) * scale
    w_values = jax.random.normal(third, (D, KV_HEADS * HEAD), jnp.float32) * scale
    w_query = jnp.clip(w_query, -6.0, 6.0)
    w_both = jnp.clip(jnp.concatenate([w_keys, w_values], axis=1), -6.0, 6.0)
    return (w_query, w_both)


def draw_wq_time(key, part):
    return projection_pair(key, 11)[0].astype(jnp.bfloat16)


def draw_wkv_time(key, part):
    return projection_pair(key, 11)[1].astype(jnp.bfloat16)


def draw_wq_space(key, part):
    return projection_pair(key, 23)[0].astype(jnp.bfloat16)


def draw_wkv_space(key, part):
    return projection_pair(key, 23)[1].astype(jnp.bfloat16)


def draw_frames(key, part):
    values = jax.random.normal(key, (FRAMES, PATCHES, D), jnp.float32)
    return jnp.clip(values, -6.0, 6.0).astype(jnp.bfloat16)


def normal_values(key, extent, width, limit, kind=jnp.bfloat16):
    return jnp.clip(width * jax.random.normal(key, extent, jnp.float32), -limit, limit).astype(kind)


def setup_inputs(seed: int = 0) -> dict:
    arg_keys = jax.random.split(jax.random.key(seed), 13)
    return {
        "frames": draw_frames(jax.random.fold_in(arg_keys[12], 71), 0),
        "gain_time": jnp.clip(1.0 + 0.15 * jax.random.normal(arg_keys[1], (D,), jnp.float32), 0.25, 1.75),
        "wq_time": draw_wq_time(jax.random.fold_in(arg_keys[12], 71), 0),
        "wkv_time": draw_wkv_time(jax.random.fold_in(arg_keys[12], 71), 0),
        "wo_time": normal_values(arg_keys[4], (HEADS * HEAD, D), D ** -0.5, 0.21875),
        "gain_space": jnp.clip(1.0 + 0.15 * jax.random.normal(arg_keys[5], (D,), jnp.float32), 0.25, 1.75),
        "wq_space": draw_wq_space(jax.random.fold_in(arg_keys[12], 71), 0),
        "wkv_space": draw_wkv_space(jax.random.fold_in(arg_keys[12], 71), 0),
        "wo_space": normal_values(arg_keys[8], (HEADS * HEAD, D), D ** -0.5, 0.21875),
        "gain_mlp": jnp.clip(1.0 + 0.15 * jax.random.normal(arg_keys[9], (D,), jnp.float32), 0.25, 1.75),
        "w_in": normal_values(arg_keys[10], (D, FF), D ** -0.5, 0.21875),
        "w_out": normal_values(arg_keys[11], (FF, D), FF ** -0.5, 0.109375),
    }


def layer_norm(x, gain):
    xf = x.astype(jnp.float32)
    mean = lax.optimization_barrier(jnp.mean(xf, axis=-1, keepdims=True))
    var = lax.optimization_barrier(jnp.mean((xf - mean) * (xf - mean), axis=-1, keepdims=True))
    return ((xf - mean) * lax.rsqrt(var + 1e-06) * gain).astype(jnp.bfloat16)

def project(a, w):
    flat = a.reshape(-1, a.shape[-1])
    return jnp.dot(flat, w, preferred_element_type=jnp.float32).reshape(a.shape[:-1] + (w.shape[1],))

def attend_time(query, keys, valid):
    group = HEADS // KV_HEADS
    patches = query.shape[0]
    span = keys.shape[0]
    q_heads = query.reshape(patches, KV_HEADS, group, HEAD).astype(jnp.float32)
    k_heads = keys[..., :KV_HEADS * HEAD].reshape(span, patches, KV_HEADS, HEAD).astype(jnp.float32)
    v_heads = keys[..., KV_HEADS * HEAD:].reshape(span, patches, KV_HEADS, HEAD).astype(jnp.float32)
    scores = jnp.einsum('pgrd,jpgd->pgrj', q_heads, k_heads) / jnp.sqrt(jnp.float32(HEAD))
    scores = jnp.where(valid, scores, jnp.float32(-1e+30))
    top = lax.optimization_barrier(jnp.max(scores, axis=-1, keepdims=True))
    expo = jnp.exp(scores - top)
    weights = (expo / lax.optimization_barrier(jnp.sum(expo, axis=-1, keepdims=True))).astype(jnp.bfloat16)
    out = jnp.einsum('pgrj,jpgd->pgrd', weights.astype(jnp.float32), v_heads)
    return out.reshape(patches, HEADS * HEAD).astype(jnp.bfloat16)

def attend_space(query, keyvals):
    group = HEADS // KV_HEADS
    patches = query.shape[0]
    count = keyvals.shape[0]
    q_heads = query.reshape(patches, KV_HEADS, group, HEAD).astype(jnp.float32)
    k_heads = keyvals[:, :KV_HEADS * HEAD].reshape(count, KV_HEADS, HEAD).astype(jnp.float32)
    v_heads = keyvals[:, KV_HEADS * HEAD:].reshape(count, KV_HEADS, HEAD).astype(jnp.float32)
    scores = jnp.einsum('pgrd,kgd->grpk', q_heads, k_heads) / jnp.sqrt(jnp.float32(HEAD))
    top = lax.optimization_barrier(jnp.max(scores, axis=-1, keepdims=True))
    expo = jnp.exp(scores - top)
    weights = (expo / lax.optimization_barrier(jnp.sum(expo, axis=-1, keepdims=True))).astype(jnp.bfloat16)
    out = jnp.einsum('grpk,kgd->pgrd', weights.astype(jnp.float32), v_heads)
    return out.reshape(patches, HEADS * HEAD).astype(jnp.bfloat16)

def reference(frames, gain_time, wq_time, wkv_time, wo_time, gain_space, wq_space, wkv_space, wo_space, gain_mlp, w_in, w_out):
    total = frames.shape[0]
    span = 2 * WINDOW + 1
    normed = layer_norm(frames, gain_time)
    queries = project(normed, wq_time).astype(jnp.bfloat16)
    keyvals = project(normed, wkv_time).astype(jnp.bfloat16)
    padded = jnp.pad(keyvals, ((WINDOW, WINDOW), (0, 0), (0, 0)))

    def one_frame(index):
        keys = lax.dynamic_slice_in_dim(padded, index, span, 0)
        where = index + jnp.arange(span, dtype=jnp.int32) - WINDOW
        valid = (where >= 0) & (where < total)
        query = lax.dynamic_index_in_dim(queries, index, 0, False)
        return attend_time(query, keys, valid)
    attended = lax.map(one_frame, jnp.arange(total, dtype=jnp.int32))
    after_time = (frames.astype(jnp.float32) + project(attended, wo_time)).astype(jnp.bfloat16)
    normed = layer_norm(after_time, gain_space)
    queries = project(normed, wq_space).astype(jnp.bfloat16)
    keyvals = project(normed, wkv_space).astype(jnp.bfloat16)
    attended = lax.map(lambda pair: attend_space(pair[0], pair[1]), (queries, keyvals))
    after_space = (after_time.astype(jnp.float32) + project(attended, wo_space)).astype(jnp.bfloat16)
    normed = layer_norm(after_space, gain_mlp)
    hidden = jax.nn.gelu(project(normed, w_in), approximate=True).astype(jnp.bfloat16)
    return (after_space.astype(jnp.float32) + project(hidden, w_out)).astype(jnp.bfloat16)
```

```python
import functools

import jax
import jax.numpy as jnp
from jax import lax
from jax.experimental import pallas as pl
from jax.experimental.pallas import tpu as pltpu
from jax.sharding import PartitionSpec as P

HEADS = 12
KV_HEADS = 4
HEAD = 64
WINDOW = 8
GROUP = HEADS // KV_HEADS
PAIRS = KV_HEADS // 2
PAIR = 2 * HEAD
KV_HALF = KV_HEADS * HEAD
PATCH = 16
BF = jnp.bfloat16
F32 = jnp.float32
CHUNKS = 2


def mm(a, b):
    return jnp.dot(a, b, preferred_element_type=F32)


def mm_t(a, b):
    return lax.dot_general(a, b, (((1,), (1,)), ((), ())), preferred_element_type=F32)


def norm(x, gain):
    mean = jnp.mean(x, axis=-1, keepdims=True)
    diff = x - mean
    var = jnp.mean(diff * diff, axis=-1, keepdims=True)
    return (diff * lax.rsqrt(var + 1e-06) * gain).astype(BF)


def softmax(s):
    e = jnp.exp(s - jnp.max(s, axis=-1, keepdims=True))
    return (e * (1.0 / jnp.sum(e, axis=-1, keepdims=True))).astype(BF)


def attend(q_tiles, keyvals, pair, bias):
    rows = q_tiles[0].shape[0]
    q = jnp.concatenate(q_tiles, axis=0)
    k = keyvals[:, pair * PAIR : (pair + 1) * PAIR]
    v = keyvals[:, KV_HALF + pair * PAIR : KV_HALF + (pair + 1) * PAIR]
    low = lax.broadcasted_iota(jnp.int32, k.shape, 1) < HEAD
    zero = jnp.zeros_like(k)
    out = None
    for half in range(2):
        mask = low if half == 0 else jnp.logical_not(low)
        s = mm_t(q, jnp.where(mask, k, zero))
        if bias is not None:
            s = (s.reshape(GROUP, rows, s.shape[1]) + bias[None]).reshape(s.shape)
        o = mm(softmax(s), jnp.where(mask, v, zero))
        out = o if out is None else out + o
    out = out.astype(BF)
    return [out[j * rows : (j + 1) * rows] for j in range(GROUP)]


def qkv_kernel(x_ref, gain_ref, wq_ref, wkv_ref, q_ref, kv_ref):
    normed = norm(x_ref[...].astype(F32), gain_ref[...])
    kv_ref[...] = mm(normed, wkv_ref[...]).astype(BF)
    q_ref[...] = (mm(normed, wq_ref[...]) * (HEAD ** -0.5)).astype(BF)


def time_kernel(
    half, patches, edge_ref, x_ref, q_ref, kv_ref, halo_ref, wo_ref, gain_ref, wq_ref, wkv_ref,
    after_ref, q_out, kv_out, attn, bias_ref,
):
    count = x_ref.shape[0]
    extent = count + 2 * WINDOW
    d = x_ref.shape[2]

    @pl.when(pl.program_id(0) == 0)
    def _():
        shape = bias_ref.shape
        row = lax.broadcasted_iota(jnp.int32, shape, 0)
        col = lax.broadcasted_iota(jnp.int32, shape, 1)
        t, s = row // PATCH, col // PATCH
        ok = (row % PATCH == col % PATCH) & (s >= t) & (s <= t + 2 * WINDOW)
        edge = edge_ref[0]
        if half == 0:
            ok = ok & (s >= edge)
        else:
            ok = ok & (s < edge)
        bias_ref[...] = jnp.where(ok, 0.0, -1e30).astype(F32)

    bias = bias_ref[...]
    rows = count * PATCH
    for g in range(patches // PATCH):
        at = slice(g * PATCH, (g + 1) * PATCH)
        own, halo = kv_ref[:, at, :], halo_ref[:, at, :]
        keys = jnp.concatenate([halo, own] if half == 0 else [own, halo], axis=0)
        keys = keys.reshape(extent * PATCH, keys.shape[2])
        for pair in range(PAIRS):
            tiles = []
            for j in range(GROUP):
                c = (pair * GROUP + j) * PAIR
                tiles.append(q_ref[:, at, c : c + PAIR].reshape(rows, PAIR))
            for j, o in enumerate(attend(tiles, keys, pair, bias)):
                c = (pair * GROUP + j) * PAIR
                attn[:, at, c : c + PAIR] = o.reshape(count, PATCH, PAIR)
    total = count * patches
    y = mm(attn[...].reshape(total, d), wo_ref[...])
    after = (x_ref[...].reshape(total, d).astype(F32) + y).astype(BF)
    after_ref[...] = after.reshape(after_ref.shape)
    normed = norm(after.astype(F32), gain_ref[...])
    kv_out[...] = mm(normed, wkv_ref[...]).astype(BF).reshape(kv_out.shape)
    q_out[...] = (mm(normed, wq_ref[...]) * (HEAD ** -0.5)).astype(BF).reshape(q_out.shape)


def mlp_tail(after, attended, wo_ref, gain_ref, win_ref, wout_ref):
    x = (after.astype(F32) + mm(attended, wo_ref[...])).astype(BF)
    normed = norm(x.astype(F32), gain_ref[...])
    ff = win_ref.shape[1]
    step = ff // 4
    acc = x.astype(F32)
    out = None
    for i in range(0, ff, step):
        hidden = jax.nn.gelu(mm(normed, win_ref[:, i : i + step]), approximate=True).astype(BF)
        y = mm(hidden, wout_ref[i : i + step, :])
        out = y if out is None else out + y
    return (acc + out).astype(BF)


def space_kernel(x_ref, q_ref, kv_ref, wo_ref, gain_ref, win_ref, wout_ref, *rest):
    out_ref, attn = rest[-2:]
    count, patches, d = x_ref.shape
    shards = kv_ref.shape[0]
    for f in range(count):
        keys = kv_ref[:, f].reshape(shards * patches, kv_ref.shape[3])
        for pair in range(PAIRS):
            tiles = []
            for j in range(GROUP):
                c = (pair * GROUP + j) * PAIR
                tiles.append(q_ref[f, :, c : c + PAIR])
            for j, o in enumerate(attend(tiles, keys, pair, None)):
                c = (pair * GROUP + j) * PAIR
                attn[f, :, c : c + PAIR] = o
    total = count * patches
    out = mlp_tail(x_ref[...].reshape(total, d), attn[...].reshape(total, d), wo_ref, gain_ref, win_ref, wout_ref)
    out_ref[...] = out.reshape(out_ref.shape)


def whole(shape):
    return pl.BlockSpec(shape, lambda *_: (0,) * len(shape), pipeline_mode=pl.Buffered(1))


def pair_columns(w):
    d = w.shape[0]
    w = w.reshape(d, PAIRS, 2, GROUP, HEAD).transpose(0, 1, 3, 2, 4)
    return w.reshape(d, HEADS * HEAD)


def pair_rows(w):
    d = w.shape[1]
    w = w.reshape(PAIRS, 2, GROUP, HEAD, d).transpose(0, 2, 1, 3, 4)
    return w.reshape(HEADS * HEAD, d)


def params():
    return pltpu.CompilerParams(vmem_limit_bytes=48 << 20)


def body(
    frames, gain_time, wq_time, wkv_time, wo_time, gain_space, wq_space, wkv_space, wo_space,
    gain_mlp, w_in, w_out,
):
    count, patches, d = frames.shape
    kvw = wkv_time.shape[1]
    ff = w_in.shape[1]
    tokens = count * patches
    gains = [g.reshape(1, d) for g in (gain_time, gain_space, gain_mlp)]
    rows = 256
    q, kv = pl.pallas_call(
        qkv_kernel,
        grid=(tokens // rows,),
        in_specs=[
            pl.BlockSpec((rows, d), lambda i: (i, 0)),
            whole((1, d)), whole((d, d)), whole((d, kvw)),
        ],
        out_specs=[pl.BlockSpec((rows, d), lambda i: (i, 0)), pl.BlockSpec((rows, kvw), lambda i: (i, 0))],
        out_shape=[jax.ShapeDtypeStruct((tokens, d), BF), jax.ShapeDtypeStruct((tokens, kvw), BF)],
        compiler_params=params(),
        name="qkv_time",
    )(frames.reshape(tokens, d), gains[0], pair_columns(wq_time), wkv_time)
    q = q.reshape(count, patches, d)
    kv = kv.reshape(count, patches, kvw)

    size = lax.axis_size("tm")
    up = [(i, (i + 1) % size) for i in range(size - 1)]
    down = [(j, i) for i, j in up]
    before = lax.ppermute(kv[count - WINDOW :], "tm", up)
    behind = lax.ppermute(kv[:WINDOW], "tm", down)
    index = lax.axis_index("tm")
    part = count // CHUNKS
    first = jnp.where(index == 0, WINDOW, 0).astype(jnp.int32).reshape(1)
    last = jnp.where(index == size - 1, count, count + WINDOW).astype(jnp.int32).reshape(1)

    block = 32
    wo_t, wq_s, wo_s = pair_rows(wo_time), pair_columns(wq_space), pair_rows(wo_space)
    stages = []
    for half, (edge, halo) in enumerate(((first, before), (last, behind))):
        stages.append(pl.pallas_call(
            functools.partial(time_kernel, half, block),
            grid=(patches // block,),
            in_specs=[
                pl.BlockSpec(memory_space=pltpu.SMEM),
                pl.BlockSpec((part, block, d), lambda i, h=half: (h, i, 0)),
                pl.BlockSpec((part, block, d), lambda i, h=half: (h, i, 0)),
                pl.BlockSpec((count, block, kvw), lambda i: (0, i, 0)),
                pl.BlockSpec((WINDOW, block, kvw), lambda i: (0, i, 0)),
                whole((d, d)), whole((1, d)), whole((d, d)), whole((d, kvw)),
            ],
            out_specs=[
                pl.BlockSpec((part, block, d), lambda i: (0, i, 0)),
                pl.BlockSpec((part, block, d), lambda i: (0, i, 0)),
                pl.BlockSpec((part, block, kvw), lambda i: (0, i, 0)),
            ],
            out_shape=[
                jax.ShapeDtypeStruct((part, patches, d), BF),
                jax.ShapeDtypeStruct((part, patches, d), BF),
                jax.ShapeDtypeStruct((part, patches, kvw), BF),
            ],
            scratch_shapes=[
                pltpu.VMEM((part, block, d), BF),
                pltpu.VMEM((part * PATCH, (part + 2 * WINDOW) * PATCH), F32),
            ],
            compiler_params=params(),
            cost_estimate=pl.CostEstimate(flops=6 * 10**9, bytes_accessed=8 << 20, transcendentals=2 << 20),
            name="time_block",
        )(edge, frames, q, kv, halo, wo_t, gains[1], wq_s, wkv_space))

    shards = lax.axis_size("space")
    gathered = [lax.all_gather(s[2], "space", axis=0, tiled=False) for s in stages]
    fb = 4
    out = None
    for half in range(CHUNKS):
        after, q_s, _ = stages[half]
        prev = [] if out is None else [out]
        out = pl.pallas_call(
            space_kernel,
            grid=(part // fb,),
            in_specs=[
                pl.BlockSpec((fb, patches, d), lambda i: (i, 0, 0)),
                pl.BlockSpec((fb, patches, d), lambda i: (i, 0, 0)),
                pl.BlockSpec((shards, fb, patches, kvw), lambda i: (0, i, 0, 0)),
                whole((d, d)), whole((1, d)), whole((d, ff)), whole((ff, d)),
            ] + [pl.BlockSpec(memory_space=pl.ANY) for _ in prev],
            out_specs=pl.BlockSpec((fb, patches, d), lambda i, h=half: (i + h * (part // fb), 0, 0)),
            out_shape=jax.ShapeDtypeStruct((count, patches, d), BF),
            scratch_shapes=[pltpu.VMEM((fb, patches, d), BF)],
            input_output_aliases={7: 0} if prev else {},
            compiler_params=params(),
            cost_estimate=pl.CostEstimate(flops=8 * 10**9, bytes_accessed=18 << 20, transcendentals=4 << 20),
            name="space_block",
        )(after, q_s, gathered[half], wo_s, gains[2], w_in, w_out, *prev)
    return out


def solution(mesh):
    in_specs = (P("tm", "space", None),) + (P(),) * 11
    out_specs = P("tm", "space", None)
    return jax.shard_map(body, mesh=mesh, in_specs=in_specs, out_specs=out_specs, check_vma=False)
```

```python
import functools

import jax
import jax.numpy as jnp
from jax import lax
from jax.experimental import pallas as pl
from jax.experimental.pallas import tpu as pltpu
from jax.sharding import PartitionSpec as P

HEADS = 12
KV_HEADS = 4
HEAD = 64
WINDOW = 8
GROUP = HEADS // KV_HEADS
PAIRS = KV_HEADS // 2
PAIR = 2 * HEAD
KV_HALF = KV_HEADS * HEAD
PATCH = 16
BF = jnp.bfloat16
F32 = jnp.float32
HALVES = 2
BLOCK = 4
MESH = pl.DeviceIdType.MESH


def mm(a, b):
    return jnp.dot(a, b, preferred_element_type=F32)


def mm_t(a, b):
    return lax.dot_general(a, b, (((1,), (1,)), ((), ())), preferred_element_type=F32)


def norm(x, gain):
    mean = jnp.mean(x, axis=-1, keepdims=True)
    diff = x - mean
    var = jnp.mean(diff * diff, axis=-1, keepdims=True)
    return (diff * lax.rsqrt(var + 1e-06) * gain).astype(BF)


def softmax(s):
    e = jnp.exp(s - jnp.max(s, axis=-1, keepdims=True))
    return (e * (1.0 / jnp.sum(e, axis=-1, keepdims=True))).astype(BF)


def attend(q_tiles, keyvals, pair, bias):
    rows = q_tiles[0].shape[0]
    q = jnp.concatenate(q_tiles, axis=0)
    k = keyvals[:, pair * PAIR : (pair + 1) * PAIR]
    v = keyvals[:, KV_HALF + pair * PAIR : KV_HALF + (pair + 1) * PAIR]
    low = lax.broadcasted_iota(jnp.int32, k.shape, 1) < HEAD
    zero = jnp.zeros_like(k)
    out = None
    for half in range(2):
        mask = low if half == 0 else jnp.logical_not(low)
        s = mm_t(q, jnp.where(mask, k, zero))
        if bias is not None:
            s = (s.reshape(GROUP, rows, s.shape[1]) + bias[None]).reshape(s.shape)
        o = mm(softmax(s), jnp.where(mask, v, zero))
        out = o if out is None else out + o
    out = out.astype(BF)
    return [out[j * rows : (j + 1) * rows] for j in range(GROUP)]


def gelu_mlp(normed, win_ref, wout_ref):
    ff = win_ref.shape[1]
    step = ff // 4
    out = None
    for i in range(0, ff, step):
        hidden = jax.nn.gelu(mm(normed, win_ref[:, i : i + step]), approximate=True).astype(BF)
        y = mm(hidden, wout_ref[i : i + step, :])
        out = y if out is None else out + y
    return out


def pair_order():
    return [(p * 2 + b) * GROUP + j for p in range(PAIRS) for j in range(GROUP) for b in range(2)]


def pair_columns(src, dst):
    order = pair_order()
    for i in range(0, HEADS, 2):
        halves = [src[:, h * HEAD : (h + 1) * HEAD] for h in order[i : i + 2]]
        dst[:, i * HEAD : (i + 2) * HEAD] = jnp.concatenate(halves, axis=1)


def kernel(
    shards,
    x_hbm, gt_ref, wqt_hbm, wkvt_hbm, wot_hbm, gs_ref, wqs_hbm, wkvs_hbm, wos_hbm, gm_ref, win_hbm, wout_hbm,
    out_hbm,
    x, raw, wqt, wkvt, wot, wqs, wkvs, wos, win, wout,
    q, kv, before, behind, attn, after, gathered, bias_ref, outs,
    in_sem, row_sem, out_sem, halo_send, halo_recv, right_send, left_send, left_recv, right_recv,
):
    count, patches, d = x.shape
    tm, size = lax.axis_index("tm"), lax.axis_size("tm")
    me = lax.axis_index("space")
    groups = patches // PATCH
    part = count // HALVES
    blocks = count // BLOCK
    extent = part + 2 * WINDOW
    nxt, prv = lax.rem(tm + 1, size), lax.rem(tm + size - 1, size)

    loads = [
        pltpu.make_async_copy(s, t, in_sem.at[i])
        for i, (s, t) in enumerate((
            (x_hbm, x), (wkvt_hbm, wkvt), (wqt_hbm, raw.at[0]), (wqs_hbm, raw.at[1]),
            (wkvs_hbm, wkvs), (win_hbm, win), (wout_hbm, wout),
        ))
    ]
    order = pair_order()

    def rows_in(src, dst, n):
        return [
            pltpu.make_async_copy(
                src.at[h * HEAD : (h + 1) * HEAD], dst.at[i * HEAD : (i + 1) * HEAD], row_sem.at[n, i]
            )
            for i, h in enumerate(order)
        ]

    wo_loads = [rows_in(wot_hbm, wot, 0), rows_in(wos_hbm, wos, 1)]
    for c in loads[:4]:
        c.start()
    for c in wo_loads[0]:
        c.start()
    for c in loads[4:5]:
        c.start()

    barrier = pltpu.get_barrier_semaphore()
    for other in (nxt, prv):
        pl.semaphore_signal(barrier, inc=1, device_id={"tm": other}, device_id_type=MESH)

    @pl.when(me > 0)
    def _():
        pl.semaphore_signal(barrier, inc=1, device_id={"space": me - 1}, device_id_type=MESH)

    @pl.when(me < shards - 1)
    def _():
        pl.semaphore_signal(barrier, inc=1, device_id={"space": me + 1}, device_id_type=MESH)

    loads[0].wait()
    loads[1].wait()
    chunk = BLOCK

    def kv_step(i, _):
        at = pl.ds(i * chunk, chunk)
        normed = norm(x[at].reshape(chunk * patches, d).astype(F32), gt_ref[...])
        attn[at] = normed.reshape(chunk, patches, d)
        kv[at] = mm(normed, wkvt[...]).astype(BF).reshape(chunk, patches, kv.shape[2])
        return 0

    lax.fori_loop(0, count // chunk, kv_step, 0)

    inner = (me > 0) & (me < shards - 1)

    @pl.when(inner)
    def _():
        pl.semaphore_wait(barrier, 4)

    @pl.when(jnp.logical_not(inner))
    def _():
        pl.semaphore_wait(barrier, 3)

    def halo_copy(side, g):
        at = slice(g * PATCH, (g + 1) * PATCH)
        src = kv.at[count - WINDOW :, at] if side == 0 else kv.at[:WINDOW, at]
        dst = before.at[:, at] if side == 0 else behind.at[:, at]
        return pltpu.make_async_remote_copy(
            src_ref=src, dst_ref=dst, send_sem=halo_send.at[side, g], recv_sem=halo_recv.at[side, g],
            device_id={"tm": nxt if side == 0 else prv}, device_id_type=MESH,
        )

    halos = [[halo_copy(side, g) for g in range(groups)] for side in range(2)]
    for side in range(2):
        for c in halos[side]:
            c.start()

    loads[2].wait()
    pair_columns(raw.at[0], wqt)

    def q_step(i, _):
        at = pl.ds(i * chunk, chunk)
        y = mm(attn[at].reshape(chunk * patches, d), wqt[...]) * (HEAD ** -0.5)
        q[at] = y.astype(BF).reshape(chunk, patches, d)
        return 0

    lax.fori_loop(0, count // chunk, q_step, 0)
    loads[3].wait()
    pair_columns(raw.at[1], wqs)
    for c in wo_loads[1] + loads[5:]:
        c.start()

    def piece(shard, b):
        return gathered.at[shard, b * BLOCK : (b + 1) * BLOCK]

    def to_right(b, dist):
        return pltpu.make_async_remote_copy(
            src_ref=piece(me - dist, b), dst_ref=piece(me - dist, b),
            send_sem=right_send.at[b, dist], recv_sem=left_recv.at[b, dist],
            device_id={"space": me + 1}, device_id_type=MESH,
        )

    def to_left(b, dist):
        return pltpu.make_async_remote_copy(
            src_ref=piece(me + dist, b), dst_ref=piece(me + dist, b),
            send_sem=left_send.at[b, dist], recv_sem=right_recv.at[b, dist],
            device_id={"space": me - 1}, device_id_type=MESH,
        )

    def send_right(b, dist):
        @pl.when((me - dist >= 0) & (me + 1 < shards))
        def _():
            to_right(b, dist).start()

    def send_left(b, dist):
        @pl.when((me + dist < shards) & (me > 0))
        def _():
            to_left(b, dist).start()

    def forward(b, dist):
        @pl.when(me - dist >= 0)
        def _():
            pltpu.make_async_remote_copy(
                src_ref=piece(me - dist, b), dst_ref=piece(me - dist, b),
                send_sem=right_send.at[b, dist - 1], recv_sem=left_recv.at[b, dist - 1],
                device_id={"space": me - 1}, device_id_type=MESH,
            ).wait_recv()

        if dist < shards - 1:
            send_right(b, dist)

        @pl.when(me + dist < shards)
        def _():
            pltpu.make_async_remote_copy(
                src_ref=piece(me + dist, b), dst_ref=piece(me + dist, b),
                send_sem=left_send.at[b, dist - 1], recv_sem=right_recv.at[b, dist - 1],
                device_id={"space": me + 1}, device_id_type=MESH,
            ).wait_recv()

        if dist < shards - 1:
            send_left(b, dist)

    pending = [(b, dist) for b0 in range(0, blocks, 2) for dist in range(1, shards) for b in (b0, b0 + 1)]
    done = []

    def advance(n=1, until=None):
        while pending and (n > 0 or (until is not None and pending_has(until))):
            b, dist = pending.pop(0)
            forward(b, dist)
            done.append((b, dist))
            n -= 1

    def pending_has(b):
        return any(e[0] == b for e in pending)

    row_t = lax.broadcasted_iota(jnp.int32, bias_ref.shape, 0)
    col_t = lax.broadcasted_iota(jnp.int32, bias_ref.shape, 1)
    for half in range(HALVES):
        first = half * part
        rt, cs = row_t // PATCH, col_t // PATCH
        ok = (row_t % PATCH == col_t % PATCH) & (cs >= rt) & (cs <= rt + 2 * WINDOW)
        if half == 0:
            ok = ok & (cs >= jnp.where(tm == 0, WINDOW, 0))
        else:
            ok = ok & (cs < jnp.where(tm == size - 1, count, count + WINDOW))
        bias_ref[...] = jnp.where(ok, 0.0, -1e30).astype(F32)
        halo_ref = before if half == 0 else behind

        for g in range(groups):
            halos[half][g].wait_recv()

        def group_step(g, _):
            at = pl.ds(pl.multiple_of(g * PATCH, PATCH), PATCH)
            own, halo = kv[:, at, :], halo_ref[:, at, :]
            keys = jnp.concatenate([halo, own] if half == 0 else [own, halo], axis=0)
            keys = keys.reshape(extent * PATCH, keys.shape[2])
            bias = bias_ref[...]
            for pair in range(PAIRS):
                tiles = []
                for j in range(GROUP):
                    c = (pair * GROUP + j) * PAIR
                    tiles.append(q[first : first + part, at, c : c + PAIR].reshape(part * PATCH, PAIR))
                for j, o in enumerate(attend(tiles, keys, pair, bias)):
                    c = (pair * GROUP + j) * PAIR
                    attn[first : first + part, at, c : c + PAIR] = o.reshape(part, PATCH, PAIR)
            return 0

        if half == 0:
            lax.fori_loop(0, groups, group_step, 0)
            for c in wo_loads[0]:
                c.wait()
            loads[4].wait()
        else:
            lax.fori_loop(0, groups // 2, group_step, 0)
            advance(1)
            lax.fori_loop(groups // 2, groups, group_step, 0)
            advance(1)

        for b in range(first // BLOCK, (first + part) // BLOCK):
            at = slice(b * BLOCK, (b + 1) * BLOCK)
            y = mm(attn[at].reshape(BLOCK * patches, d), wot[...])
            res = (x[at].reshape(BLOCK * patches, d).astype(F32) + y).astype(BF)
            after[at] = res.reshape(BLOCK, patches, d)
            normed = norm(res.astype(F32), gs_ref[...])
            keyvals = mm(normed, wkvs[...]).astype(BF)
            gathered[me, at] = keyvals.reshape(BLOCK, patches, keyvals.shape[1])
            send_right(b, 0)
            send_left(b, 0)
            y = mm(normed, wqs[...]) * (HEAD ** -0.5)
            q[at] = y.astype(BF).reshape(BLOCK, patches, d)

    for c in wo_loads[1] + loads[5:]:
        c.wait()
    writes = []
    for b in range(blocks):
        advance(0, until=b)
        at = slice(b * BLOCK, (b + 1) * BLOCK)

        def frame_step(i, _):
            f = b * BLOCK + i
            keys = gathered[:, f].reshape(shards * patches, gathered.shape[3])
            for pair in range(PAIRS):
                tiles = []
                for j in range(GROUP):
                    c = (pair * GROUP + j) * PAIR
                    tiles.append(q[f, :, c : c + PAIR])
                for j, o in enumerate(attend(tiles, keys, pair, None)):
                    c = (pair * GROUP + j) * PAIR
                    attn[f, :, c : c + PAIR] = o
            return 0

        lax.fori_loop(0, BLOCK // 2, frame_step, 0)
        advance(1)
        lax.fori_loop(BLOCK // 2, BLOCK, frame_step, 0)
        advance(1)
        y = mm(attn[at].reshape(BLOCK * patches, d), wos[...])
        res = (after[at].reshape(BLOCK * patches, d).astype(F32) + y).astype(BF)
        normed = norm(res.astype(F32), gm_ref[...])
        y = (res.astype(F32) + gelu_mlp(normed, win, wout)).astype(BF)
        outs[at] = y.reshape(BLOCK, patches, d)
        write = pltpu.make_async_copy(outs.at[at], out_hbm.at[at], out_sem.at[b])
        write.start()
        writes.append(write)
        advance(1)

    for c in writes:
        c.wait()
    for side in range(2):
        for c in halos[side]:
            c.wait_send()
    for b in range(blocks):
        for dist in range(shards - 1):
            @pl.when((me - dist >= 0) & (me + 1 < shards))
            def _():
                to_right(b, dist).wait_send()

            @pl.when((me + dist < shards) & (me > 0))
            def _():
                to_left(b, dist).wait_send()


def body(*args):
    frames, gain_time, wq_time, wkv_time, wo_time, gain_space, wq_space, wkv_space, wo_space, gain_mlp, w_in, w_out = args
    count, patches, d = frames.shape
    kvw = wkv_time.shape[1]
    ff = w_in.shape[1]
    shards = lax.axis_size("space")
    gains = [g.reshape(1, d) for g in (gain_time, gain_space, gain_mlp)]
    part = count // HALVES
    blocks = count // BLOCK
    groups = patches // PATCH
    hbm = pl.BlockSpec(memory_space=pl.ANY)
    vmem = pl.BlockSpec(memory_space=pltpu.VMEM)
    dma = pltpu.SemaphoreType.DMA
    return pl.pallas_call(
        functools.partial(kernel, shards),
        in_specs=[hbm, vmem, hbm, hbm, hbm, vmem, hbm, hbm, hbm, vmem, hbm, hbm],
        out_specs=hbm,
        out_shape=jax.ShapeDtypeStruct(frames.shape, BF),
        scratch_shapes=[
            pltpu.VMEM((count, patches, d), BF),
            pltpu.VMEM((2, d, d), BF),
            pltpu.VMEM((d, d), BF),
            pltpu.VMEM((d, kvw), BF),
            pltpu.VMEM((d, d), BF),
            pltpu.VMEM((d, d), BF),
            pltpu.VMEM((d, kvw), BF),
            pltpu.VMEM((d, d), BF),
            pltpu.VMEM((d, ff), BF),
            pltpu.VMEM((ff, d), BF),
            pltpu.VMEM((count, patches, d), BF),
            pltpu.VMEM((count, patches, kvw), BF),
            pltpu.VMEM((WINDOW, patches, kvw), BF),
            pltpu.VMEM((WINDOW, patches, kvw), BF),
            pltpu.VMEM((count, patches, d), BF),
            pltpu.VMEM((count, patches, d), BF),
            pltpu.VMEM((shards, count, patches, kvw), BF),
            pltpu.VMEM((part * PATCH, (part + 2 * WINDOW) * PATCH), F32),
            pltpu.VMEM((count, patches, d), BF),
            dma((7,)),
            dma((2, HEADS)),
            dma((blocks,)),
            dma((2, groups)),
            dma((2, groups)),
            dma((blocks, shards)),
            dma((blocks, shards)),
            dma((blocks, shards)),
            dma((blocks, shards)),
        ],
        compiler_params=pltpu.CompilerParams(
            vmem_limit_bytes=60 << 20, collective_id=0, has_side_effects=True
        ),
        name="encoder_block",
    )(frames, gains[0], wq_time, wkv_time, wo_time, gains[1], wq_space, wkv_space, wo_space, gains[2], w_in, w_out)


def solution(mesh):
    in_specs = (P("tm", "space", None),) + (P(),) * 11
    out_specs = P("tm", "space", None)
    return jax.shard_map(body, mesh=mesh, in_specs=in_specs, out_specs=out_specs, check_vma=False)
```

```python
import functools

import jax
import jax.numpy as jnp
from jax import lax
from jax.experimental import pallas as pl
from jax.experimental.pallas import tpu as pltpu
from jax.sharding import PartitionSpec as P

HEADS = 12
KV_HEADS = 4
HEAD = 64
WINDOW = 8
GROUP = HEADS // KV_HEADS
PAIRS = KV_HEADS // 2
PAIR = 2 * HEAD
KV_HALF = KV_HEADS * HEAD
PATCH = 16
BF = jnp.bfloat16
F32 = jnp.float32
HALVES = 2
BLOCK = 4
MESH = pl.DeviceIdType.MESH


def mm(a, b):
    return jnp.dot(a, b, preferred_element_type=F32)


def mm_t(a, b):
    return lax.dot_general(a, b, (((1,), (1,)), ((), ())), preferred_element_type=F32)


def norm(x, gain):
    mean = jnp.mean(x, axis=-1, keepdims=True)
    diff = x - mean
    var = jnp.mean(diff * diff, axis=-1, keepdims=True)
    return (diff * lax.rsqrt(var + 1e-06) * gain).astype(BF)


def softmax(s):
    e = jnp.exp(s - jnp.max(s, axis=-1, keepdims=True))
    return (e * (1.0 / jnp.sum(e, axis=-1, keepdims=True))).astype(BF)


def attend(q_tiles, keyvals, pair, bias):
    rows = q_tiles[0].shape[0]
    q = jnp.concatenate(q_tiles, axis=0)
    k = keyvals[:, pair * PAIR : (pair + 1) * PAIR]
    v = keyvals[:, KV_HALF + pair * PAIR : KV_HALF + (pair + 1) * PAIR]
    low = lax.broadcasted_iota(jnp.int32, k.shape, 1) < HEAD
    zero = jnp.zeros_like(k)
    out = None
    for half in range(2):
        mask = low if half == 0 else jnp.logical_not(low)
        s = mm_t(q, jnp.where(mask, k, zero))
        if bias is not None:
            s = (s.reshape(GROUP, rows, s.shape[1]) + bias[None]).reshape(s.shape)
        o = mm(softmax(s), jnp.where(mask, v, zero))
        out = o if out is None else out + o
    out = out.astype(BF)
    return [out[j * rows : (j + 1) * rows] for j in range(GROUP)]


def gelu_mlp(normed, win_ref, wout_ref):
    ff = win_ref.shape[1]
    step = ff // 4
    out = None
    for i in range(0, ff, step):
        hidden = jax.nn.gelu(mm(normed, win_ref[:, i : i + step]), approximate=True).astype(BF)
        y = mm(hidden, wout_ref[i : i + step, :])
        out = y if out is None else out + y
    return out


def pair_order():
    return [(p * 2 + b) * GROUP + j for p in range(PAIRS) for j in range(GROUP) for b in range(2)]


def pair_columns(src, dst):
    order = pair_order()
    for i in range(0, HEADS, 2):
        halves = [src[:, h * HEAD : (h + 1) * HEAD] for h in order[i : i + 2]]
        dst[:, i * HEAD : (i + 2) * HEAD] = jnp.concatenate(halves, axis=1)


def kernel(
    shards,
    x_hbm, gt_ref, wqt_hbm, wkvt_hbm, wot_hbm, gs_ref, wqs_hbm, wkvs_hbm, wos_hbm, gm_ref, win_hbm, wout_hbm,
    out_hbm,
    x, raw, wqt, wkvt, wot, wqs, wkvs, wos, win, wout,
    q, kv, before, behind, attn, after, gathered, bias_ref, outs,
    q_in, host_out, returned,
    in_sem, row_sem, out_sem, halo_send, halo_recv, right_send, left_send, left_recv, right_recv,
    q_send, q_recv, back_send, back_recv,
):
    count, patches, d = x.shape
    tm, size = lax.axis_index("tm"), lax.axis_size("tm")
    me = lax.axis_index("space")
    groups = patches // PATCH
    part = count // HALVES
    blocks = count // BLOCK
    extent = part + 2 * WINDOW
    hosted = blocks // 2 if shards >= 4 else 0
    is_end = (me == 0) | (me == shards - 1)
    is_host = (me == 1) | (me == shards - 2)
    nxt, prv = lax.rem(tm + 1, size), lax.rem(tm + size - 1, size)

    loads = [
        pltpu.make_async_copy(s, t, in_sem.at[i])
        for i, (s, t) in enumerate((
            (x_hbm, x), (wkvt_hbm, wkvt), (wqt_hbm, raw.at[0]), (wqs_hbm, raw.at[1]),
            (wkvs_hbm, wkvs), (win_hbm, win), (wout_hbm, wout),
        ))
    ]
    order = pair_order()

    def rows_in(src, dst, n):
        return [
            pltpu.make_async_copy(
                src.at[h * HEAD : (h + 1) * HEAD], dst.at[i * HEAD : (i + 1) * HEAD], row_sem.at[n, i]
            )
            for i, h in enumerate(order)
        ]

    wo_loads = [rows_in(wot_hbm, wot, 0), rows_in(wos_hbm, wos, 1)]
    for c in loads[:4]:
        c.start()
    for c in wo_loads[0]:
        c.start()
    for c in loads[4:5]:
        c.start()

    barrier = pltpu.get_barrier_semaphore()
    for other in (nxt, prv):
        pl.semaphore_signal(barrier, inc=1, device_id={"tm": other}, device_id_type=MESH)

    @pl.when(me > 0)
    def _():
        pl.semaphore_signal(barrier, inc=1, device_id={"space": me - 1}, device_id_type=MESH)

    @pl.when(me < shards - 1)
    def _():
        pl.semaphore_signal(barrier, inc=1, device_id={"space": me + 1}, device_id_type=MESH)

    loads[0].wait()
    loads[1].wait()
    chunk = BLOCK

    def kv_step(i, _):
        at = pl.ds(i * chunk, chunk)
        normed = norm(x[at].reshape(chunk * patches, d).astype(F32), gt_ref[...])
        attn[at] = normed.reshape(chunk, patches, d)
        kv[at] = mm(normed, wkvt[...]).astype(BF).reshape(chunk, patches, kv.shape[2])
        return 0

    lax.fori_loop(0, count // chunk, kv_step, 0)

    inner = (me > 0) & (me < shards - 1)

    @pl.when(inner)
    def _():
        pl.semaphore_wait(barrier, 4)

    @pl.when(jnp.logical_not(inner))
    def _():
        pl.semaphore_wait(barrier, 3)

    def halo_copy(side, g):
        at = slice(g * PATCH, (g + 1) * PATCH)
        src = kv.at[count - WINDOW :, at] if side == 0 else kv.at[:WINDOW, at]
        dst = before.at[:, at] if side == 0 else behind.at[:, at]
        return pltpu.make_async_remote_copy(
            src_ref=src, dst_ref=dst, send_sem=halo_send.at[side, g], recv_sem=halo_recv.at[side, g],
            device_id={"tm": nxt if side == 0 else prv}, device_id_type=MESH,
        )

    halos = [[halo_copy(side, g) for g in range(groups)] for side in range(2)]
    for side in range(2):
        for c in halos[side]:
            c.start()

    loads[2].wait()
    pair_columns(raw.at[0], wqt)

    def q_step(i, _):
        at = pl.ds(i * chunk, chunk)
        y = mm(attn[at].reshape(chunk * patches, d), wqt[...]) * (HEAD ** -0.5)
        q[at] = y.astype(BF).reshape(chunk, patches, d)
        return 0

    lax.fori_loop(0, count // chunk, q_step, 0)
    loads[3].wait()
    pair_columns(raw.at[1], wqs)
    for c in wo_loads[1] + loads[5:]:
        c.start()

    def piece(shard, b):
        return gathered.at[shard, b * BLOCK : (b + 1) * BLOCK]

    def to_right(b, dist):
        return pltpu.make_async_remote_copy(
            src_ref=piece(me - dist, b), dst_ref=piece(me - dist, b),
            send_sem=right_send.at[b, dist], recv_sem=left_recv.at[b, dist],
            device_id={"space": me + 1}, device_id_type=MESH,
        )

    def to_left(b, dist):
        return pltpu.make_async_remote_copy(
            src_ref=piece(me + dist, b), dst_ref=piece(me + dist, b),
            send_sem=left_send.at[b, dist], recv_sem=right_recv.at[b, dist],
            device_id={"space": me - 1}, device_id_type=MESH,
        )

    def sends_right(b, dist):
        return (me - dist >= 0) & (me + (2 if b < hosted else 1) < shards)

    def sends_left(b, dist):
        return (me + dist < shards) & (me > (1 if b < hosted else 0))

    def query_copy(b, step):
        at = slice(b * BLOCK, (b + 1) * BLOCK)
        return pltpu.make_async_remote_copy(
            src_ref=q.at[at], dst_ref=q_in.at[at], send_sem=q_send.at[b], recv_sem=q_recv.at[b],
            device_id={"space": me + step}, device_id_type=MESH,
        )

    def back_copy(b, step):
        at = slice(b * BLOCK, (b + 1) * BLOCK)
        return pltpu.make_async_remote_copy(
            src_ref=host_out.at[at], dst_ref=returned.at[at], send_sem=back_send.at[b], recv_sem=back_recv.at[b],
            device_id={"space": me + step}, device_id_type=MESH,
        )

    def on(position, action):
        @pl.when(me == position)
        def _():
            action()

    def send_right(b, dist):
        @pl.when(sends_right(b, dist))
        def _():
            to_right(b, dist).start()

    def send_left(b, dist):
        @pl.when(sends_left(b, dist))
        def _():
            to_left(b, dist).start()

    def forward(b, dist):
        @pl.when((me - dist >= 0) & (me < shards - (1 if b < hosted else 0)))
        def _():
            pltpu.make_async_remote_copy(
                src_ref=piece(me - dist, b), dst_ref=piece(me - dist, b),
                send_sem=right_send.at[b, dist - 1], recv_sem=left_recv.at[b, dist - 1],
                device_id={"space": me - 1}, device_id_type=MESH,
            ).wait_recv()

        if dist < shards - 1:
            send_right(b, dist)

        @pl.when((me + dist < shards) & (me >= (1 if b < hosted else 0)))
        def _():
            pltpu.make_async_remote_copy(
                src_ref=piece(me + dist, b), dst_ref=piece(me + dist, b),
                send_sem=left_send.at[b, dist - 1], recv_sem=right_recv.at[b, dist - 1],
                device_id={"space": me + 1}, device_id_type=MESH,
            ).wait_recv()

        if dist < shards - 1:
            send_left(b, dist)

    pending = [(b, dist) for b0 in range(0, blocks, 2) for dist in range(1, shards) for b in (b0, b0 + 1)]
    done = []

    def advance(n=1, until=None):
        while pending and (n > 0 or (until is not None and pending_has(until))):
            b, dist = pending.pop(0)
            forward(b, dist)
            done.append((b, dist))
            n -= 1

    def pending_has(b):
        return any(e[0] == b for e in pending)

    row_t = lax.broadcasted_iota(jnp.int32, bias_ref.shape, 0)
    col_t = lax.broadcasted_iota(jnp.int32, bias_ref.shape, 1)
    for half in range(HALVES):
        first = half * part
        rt, cs = row_t // PATCH, col_t // PATCH
        ok = (row_t % PATCH == col_t % PATCH) & (cs >= rt) & (cs <= rt + 2 * WINDOW)
        if half == 0:
            ok = ok & (cs >= jnp.where(tm == 0, WINDOW, 0))
        else:
            ok = ok & (cs < jnp.where(tm == size - 1, count, count + WINDOW))
        bias_ref[...] = jnp.where(ok, 0.0, -1e30).astype(F32)
        halo_ref = before if half == 0 else behind

        for g in range(groups):
            halos[half][g].wait_recv()

        def group_step(g, _):
            at = pl.ds(pl.multiple_of(g * PATCH, PATCH), PATCH)
            own, halo = kv[:, at, :], halo_ref[:, at, :]
            keys = jnp.concatenate([halo, own] if half == 0 else [own, halo], axis=0)
            keys = keys.reshape(extent * PATCH, keys.shape[2])
            bias = bias_ref[...]
            for pair in range(PAIRS):
                tiles = []
                for j in range(GROUP):
                    c = (pair * GROUP + j) * PAIR
                    tiles.append(q[first : first + part, at, c : c + PAIR].reshape(part * PATCH, PAIR))
                for j, o in enumerate(attend(tiles, keys, pair, bias)):
                    c = (pair * GROUP + j) * PAIR
                    attn[first : first + part, at, c : c + PAIR] = o.reshape(part, PATCH, PAIR)
            return 0

        if half == 0:
            lax.fori_loop(0, groups, group_step, 0)
            for c in wo_loads[0]:
                c.wait()
            loads[4].wait()
        else:
            lax.fori_loop(0, groups // 2, group_step, 0)
            advance(1)
            lax.fori_loop(groups // 2, groups, group_step, 0)
            advance(1)

        for b in range(first // BLOCK, (first + part) // BLOCK):
            at = slice(b * BLOCK, (b + 1) * BLOCK)
            y = mm(attn[at].reshape(BLOCK * patches, d), wot[...])
            res = (x[at].reshape(BLOCK * patches, d).astype(F32) + y).astype(BF)
            after[at] = res.reshape(BLOCK, patches, d)
            normed = norm(res.astype(F32), gs_ref[...])
            keyvals = mm(normed, wkvs[...]).astype(BF)
            gathered[me, at] = keyvals.reshape(BLOCK, patches, keyvals.shape[1])
            send_right(b, 0)
            send_left(b, 0)
            y = mm(normed, wqs[...]) * (HEAD ** -0.5)
            q[at] = y.astype(BF).reshape(BLOCK, patches, d)
            if b < hosted:
                on(0, lambda: query_copy(b, 1).start())
                on(shards - 1, lambda: query_copy(b, -1).start())

    for c in wo_loads[1] + loads[5:]:
        c.wait()
    writes = []
    for b in range(blocks):
        advance(0, until=b)
        at = slice(b * BLOCK, (b + 1) * BLOCK)

        def attention(source, target, start, stop):
            def frame_step(i, _):
                f = b * BLOCK + i
                keys = gathered[:, f].reshape(shards * patches, gathered.shape[3])
                for pair in range(PAIRS):
                    tiles = []
                    for j in range(GROUP):
                        c = (pair * GROUP + j) * PAIR
                        tiles.append(source[f, :, c : c + PAIR])
                    for j, o in enumerate(attend(tiles, keys, pair, None)):
                        c = (pair * GROUP + j) * PAIR
                        target[f, :, c : c + PAIR] = o
                return 0

            lax.fori_loop(start, stop, frame_step, 0)

        if b < hosted:
            @pl.when(is_host)
            def _():
                query_copy(b, 1).wait_recv()
                attention(q_in, host_out, 0, BLOCK)

            on(1, lambda: back_copy(b, -1).start())
            on(shards - 2, lambda: back_copy(b, 1).start())
            advance(1)

            @pl.when(jnp.logical_not(is_end))
            def _():
                attention(q, attn, 0, BLOCK)

            advance(1)

            on(0, lambda: back_copy(b, 1).wait_recv())
            on(shards - 1, lambda: back_copy(b, -1).wait_recv())

            @pl.when(is_end)
            def _():
                attn[at] = returned[at]
        else:
            attention(q, attn, 0, BLOCK // 2)
            advance(1)
            attention(q, attn, BLOCK // 2, BLOCK)
            advance(1)
        y = mm(attn[at].reshape(BLOCK * patches, d), wos[...])
        res = (after[at].reshape(BLOCK * patches, d).astype(F32) + y).astype(BF)
        normed = norm(res.astype(F32), gm_ref[...])
        y = (res.astype(F32) + gelu_mlp(normed, win, wout)).astype(BF)
        outs[at] = y.reshape(BLOCK, patches, d)
        write = pltpu.make_async_copy(outs.at[at], out_hbm.at[at], out_sem.at[b])
        write.start()
        writes.append(write)
        advance(1)

    for c in writes:
        c.wait()
    for side in range(2):
        for c in halos[side]:
            c.wait_send()
    for b in range(blocks):
        for dist in range(shards - 1):
            @pl.when(sends_right(b, dist))
            def _():
                to_right(b, dist).wait_send()

            @pl.when(sends_left(b, dist))
            def _():
                to_left(b, dist).wait_send()

    for b in range(hosted):
        on(0, lambda: query_copy(b, 1).wait_send())
        on(shards - 1, lambda: query_copy(b, -1).wait_send())
        on(1, lambda: back_copy(b, -1).wait_send())
        on(shards - 2, lambda: back_copy(b, 1).wait_send())


def body(*args):
    frames, gain_time, wq_time, wkv_time, wo_time, gain_space, wq_space, wkv_space, wo_space, gain_mlp, w_in, w_out = args
    count, patches, d = frames.shape
    kvw = wkv_time.shape[1]
    ff = w_in.shape[1]
    shards = lax.axis_size("space")
    gains = [g.reshape(1, d) for g in (gain_time, gain_space, gain_mlp)]
    part = count // HALVES
    blocks = count // BLOCK
    groups = patches // PATCH
    hbm = pl.BlockSpec(memory_space=pl.ANY)
    vmem = pl.BlockSpec(memory_space=pltpu.VMEM)
    dma = pltpu.SemaphoreType.DMA
    return pl.pallas_call(
        functools.partial(kernel, shards),
        in_specs=[hbm, vmem, hbm, hbm, hbm, vmem, hbm, hbm, hbm, vmem, hbm, hbm],
        out_specs=hbm,
        out_shape=jax.ShapeDtypeStruct(frames.shape, BF),
        scratch_shapes=[
            pltpu.VMEM((count, patches, d), BF),
            pltpu.VMEM((2, d, d), BF),
            pltpu.VMEM((d, d), BF),
            pltpu.VMEM((d, kvw), BF),
            pltpu.VMEM((d, d), BF),
            pltpu.VMEM((d, d), BF),
            pltpu.VMEM((d, kvw), BF),
            pltpu.VMEM((d, d), BF),
            pltpu.VMEM((d, ff), BF),
            pltpu.VMEM((ff, d), BF),
            pltpu.VMEM((count, patches, d), BF),
            pltpu.VMEM((count, patches, kvw), BF),
            pltpu.VMEM((WINDOW, patches, kvw), BF),
            pltpu.VMEM((WINDOW, patches, kvw), BF),
            pltpu.VMEM((count, patches, d), BF),
            pltpu.VMEM((count, patches, d), BF),
            pltpu.VMEM((shards, count, patches, kvw), BF),
            pltpu.VMEM((part * PATCH, (part + 2 * WINDOW) * PATCH), F32),
            pltpu.VMEM((count, patches, d), BF),
            pltpu.VMEM((part, patches, d), BF),
            pltpu.VMEM((part, patches, d), BF),
            pltpu.VMEM((part, patches, d), BF),
            dma((7,)),
            dma((2, HEADS)),
            dma((blocks,)),
            dma((2, groups)),
            dma((2, groups)),
            dma((blocks, shards)),
            dma((blocks, shards)),
            dma((blocks, shards)),
            dma((blocks, shards)),
            dma((blocks,)),
            dma((blocks,)),
            dma((blocks,)),
            dma((blocks,)),
        ],
        compiler_params=pltpu.CompilerParams(
            vmem_limit_bytes=60 << 20, collective_id=0, has_side_effects=True
        ),
        name="encoder_block",
    )(frames, gains[0], wq_time, wkv_time, wo_time, gains[1], wq_space, wkv_space, wo_space, gains[2], w_in, w_out)


def solution(mesh):
    in_specs = (P("tm", "space", None),) + (P(),) * 11
    out_specs = P("tm", "space", None)
    return jax.shard_map(body, mesh=mesh, in_specs=in_specs, out_specs=out_specs, check_vma=False)
```
